32 devices in a mesh: inp: 2 (over x), tm: 16 (over z, y, core).
Axes of the slice: x: 2, y: 2, z: 4, core: 2. Of those that a mesh axis runs over, the one named last changes fastest.
Arguments:
- samples: int32 [512, 524288], P('inp', 'tm'), may hold values from -8 to 7
- filter_taps: int32 [4, 2048], replicated, may hold values from -4096 to 4095
Outputs:
- visibilities: float32 [2, 1024, 512, 512], P(None, ('inp', 'tm'))
The draws below stay inside these ranges and needn't reach their ends.
All inputs are finite; a program needn't handle non-finite values.
Results may differ from the reference program's by a relative error of at most 0.0032.
Values may be sent and summed in bfloat16 or wider, within the bound.
No kernel may reach another device: no remote copies, remote signals or barrier semaphores. Data moves between devices by JAX's collectives and lax.ppermute only.
A program may use at most 256 MiB of HBM per device.

```python
import math
import jax
import jax.numpy as jnp
from jax import lax

NI = 512
FFT = 2048
TAPS = 4
CH = 1024
NSPEC = 256


def plant(array, rng, least, top_value):
    longest = array.shape.index(max(array.shape))
    spots = []
    for shift in (0, 1):
        where = [jax.random.randint(jax.random.fold_in(rng, axis), (), 0, length) for axis, length in enumerate(array.shape)]
        where[longest] = (where[longest] + shift) % array.shape[longest]
        spots.append(tuple(where))
    return array.at[spots[0]].set(least).at[spots[1]].set(top_value)


def setup_inputs(seed: int = 0) -> dict:
    streams_of = jax.random.split(jax.random.key(seed), 3)
    return {
        "samples": plant(jax.random.randint(streams_of[0], (NI, NSPEC * FFT), -8, 8), jax.random.fold_in(streams_of[0], 1), -8, 7).astype(jnp.int32),
        "filter_taps": plant(jax.random.randint(streams_of[1], (TAPS, FFT), -4096, 4096), jax.random.fold_in(streams_of[1], 1), -4096, 4095).astype(jnp.int32),
    }


def reference(samples, filter_taps):
    frames = samples.reshape(NI, NSPEC, FFT).astype(jnp.float32)
    padded = jnp.pad(frames, ((0, 0), (TAPS - 1, 0), (0, 0)))
    weights = filter_taps.astype(jnp.float32) / 16384.0
    filtered = jnp.zeros((NI, NSPEC, FFT), jnp.float32)
    for offset in range(TAPS):
        filtered = filtered + weights[offset] * padded[:, offset:offset + NSPEC, :]
    rounded = lax.optimization_barrier(filtered.astype(jnp.bfloat16)).astype(jnp.float32)
    spectrum = jnp.fft.rfft(rounded, axis=-1)[:, :, :CH] / math.sqrt(FFT)
    per_group = 8
    real_part = jnp.transpose(spectrum.real, (2, 0, 1)).reshape(CH // per_group, per_group, NI, NSPEC)
    imag_part = jnp.transpose(spectrum.imag, (2, 0, 1)).reshape(CH // per_group, per_group, NI, NSPEC)

    def correlate(pair):
        real_block, imag_block = pair
        highest = lax.Precision.HIGHEST
        power = jnp.einsum('cas,cbs->cab', real_block, real_block, precision=highest)
        power = power + jnp.einsum('cas,cbs->cab', imag_block, imag_block, precision=highest)
        phase = jnp.einsum('cas,cbs->cab', imag_block, real_block, precision=highest)
        phase = phase - jnp.einsum('cas,cbs->cab', real_block, imag_block, precision=highest)
        return jnp.stack([power, phase]) / NSPEC
    result = lax.map(correlate, (real_part, imag_part))
    return jnp.transpose(result, (1, 0, 2, 3, 4)).reshape(2, CH, NI, NI)
```

```python
import math

import jax
import jax.numpy as jnp
import numpy as np
from jax import lax
from jax.experimental import pallas as pl
from jax.experimental.pallas import tpu as pltpu
from jax.sharding import PartitionSpec as P

GROUPS = 8
F32 = jnp.float32
BF16 = jnp.bfloat16


def shifted(value, axis, steps):
    count = lax.axis_size(axis)
    initial, last = (max(0, -steps), min(count, count - steps))
    return lax.ppermute(value, axis, [(source, source + steps) for source in range(initial, last)])


def angle_tables(owners, chan_dev, frame_len):
    points = np.arange(frame_len)[None, :]
    coarse = (np.arange(owners)[:, None] * chan_dev * points) % frame_len
    fine = (np.arange(chan_dev)[:, None] * points) % frame_len
    turn = 2.0 * math.pi / frame_len
    return [
        np.stack([np.cos(part * turn), np.sin(part * turn)]).astype(np.float32) for part in (coarse, fine)
    ]


def build_table(coarse, fine, high, low, group, fine_count, owners):
    for j in range(fine_count):
        at = group * fine_count + j
        cos_f = fine[0, at : at + 1, :]
        sin_f = fine[1, at : at + 1, :]
        parts = (
            coarse[0] * cos_f - coarse[1] * sin_f,
            -(coarse[1] * cos_f + coarse[0] * sin_f),
        )
        for p, exact in enumerate(parts):
            rows = pl.ds((2 * j + p) * owners, owners)
            rounded = exact.astype(BF16)
            high[rows, :] = rounded
            low[rows, :] = (exact - rounded.astype(F32)).astype(BF16)


def transform(frame, high, low, spread, step, steps, fine_count, owners):
    contract = (((1,), (1,)), ((), ()))
    spectra = lax.dot_general(high[...], frame, contract, preferred_element_type=F32)
    spectra = spectra + lax.dot_general(low[...], frame, contract, preferred_element_type=F32)
    for part in range(2 * fine_count):
        piece = spectra[part * owners : (part + 1) * owners]
        for lane in range(spread.shape[0]):
            width = spread.shape[2]
            where = pl.ds(part * steps + step, owners, stride=2 * fine_count * steps)
            spread[lane, where, :] = piece[:, lane * width : (lane + 1) * width]


def flush(spread, out, owners):
    width = spread.shape[2]
    for lane in range(spread.shape[0]):
        out[:, :, lane * width : (lane + 1) * width] = (
            spread[lane].reshape(owners, -1, width).astype(BF16)
        )


def filter_kernel(samples, halo, taps, coarse, fine, filtered, out, high, low, spread, recent, *, group, fine_count, owners, steps, keep):
    step = pl.program_id(0)

    @pl.when(step == 0)
    def _():
        build_table(coarse, fine, high, low, group, fine_count, owners)
        for k in range(keep):
            recent[k] = halo[:, k * samples.shape[1] : (k + 1) * samples.shape[1]]

    weights = taps[...].astype(F32) * (1.0 / 16384.0)
    current = samples[...].astype(F32)
    total = weights[0:1] * recent[0].astype(F32)
    for k in range(1, keep):
        total = total + weights[k : k + 1] * recent[k].astype(F32)
    total = total + weights[keep : keep + 1] * current
    rounded = total.astype(BF16)
    filtered[0] = rounded
    for k in range(keep - 1):
        recent[k] = recent[k + 1]
    recent[keep - 1] = current.astype(BF16)
    transform(rounded, high, low, spread, step, steps, fine_count, owners)

    @pl.when(step == steps - 1)
    def _():
        flush(spread, out, owners)


def transform_kernel(filtered, coarse, fine, out, high, low, spread, *, group, fine_count, owners, steps):
    step = pl.program_id(0)

    @pl.when(step == 0)
    def _():
        build_table(coarse, fine, high, low, group, fine_count, owners)

    transform(filtered[0], high, low, spread, step, steps, fine_count, owners)

    @pl.when(step == steps - 1)
    def _():
        flush(spread, out, owners)


def correlate_kernel(*refs, inp_count, scale):
    arrived, out = refs[0], refs[-1]
    sources, rows, width = arrived.shape
    steps = rows // 2
    block = arrived[...]
    parts = []
    for p in range(2):
        part = block[:, p * steps : (p + 1) * steps, :]
        part = part.reshape(inp_count, (sources // inp_count) * steps, width)
        parts.append(jnp.concatenate([part[i] for i in range(inp_count)], axis=1))
    real, imag = parts
    real_t, imag_t = real.T, imag.T

    def product(left, right):
        return lax.dot_general(left, right, (((1,), (0,)), ((), ())), preferred_element_type=F32)

    out[0, 0] = (product(real_t, real) + product(imag_t, imag)) * scale
    out[1, 0] = (product(imag_t, real) - product(real_t, imag)) * scale


def on_device(samples, filter_taps):
    local_inputs = samples.shape[0]
    tap_count, frame_len = filter_taps.shape
    steps = samples.shape[1] // frame_len
    channels = frame_len // 2
    inp_count = lax.axis_size("inp")
    tm_count = lax.axis_size("tm")
    owners = inp_count * tm_count
    all_inputs = local_inputs * inp_count
    chan_dev = channels // owners
    groups = math.gcd(GROUPS, chan_dev)
    fine_count = chan_dev // groups
    total_spectra = steps * tm_count
    keep = tap_count - 1
    rows = 2 * fine_count * owners
    lane_width = min(128, local_inputs)
    lanes = local_inputs // lane_width
    coarse, fine = [jnp.asarray(t) for t in angle_tables(owners, chan_dev, frame_len)]

    tail = samples[:, (steps - keep) * frame_len :].astype(BF16)
    halo = shifted(tail, "tm", 1)

    scratch = [
        pltpu.VMEM((rows, frame_len), BF16),
        pltpu.VMEM((rows, frame_len), BF16),
        pltpu.VMEM((lanes, rows * steps, lane_width), F32),
    ]
    once = pl.Buffered(1)

    def whole(*shape):
        return pl.BlockSpec(shape, lambda s: (0,) * len(shape), pipeline_mode=once)

    piece = jax.ShapeDtypeStruct((owners, 2 * fine_count * steps, local_inputs), BF16)
    tables = [whole(*coarse.shape), whole(*fine.shape)]
    frame_spec = pl.BlockSpec((1, local_inputs, frame_len), lambda s: (s, 0, 0))
    filtered, first = pl.pallas_call(
        lambda *refs: filter_kernel(*refs, group=0, fine_count=fine_count, owners=owners, steps=steps, keep=keep),
        grid=(steps,),
        in_specs=[
            pl.BlockSpec((local_inputs, frame_len), lambda s: (0, s)),
            whole(local_inputs, keep * frame_len),
            whole(tap_count, frame_len),
            *tables,
        ],
        out_specs=[frame_spec, whole(*piece.shape)],
        out_shape=[jax.ShapeDtypeStruct((steps, local_inputs, frame_len), BF16), piece],
        scratch_shapes=scratch + [pltpu.VMEM((keep, local_inputs, frame_len), BF16)],
        name="filter_transform",
    )(samples, halo, filter_taps, coarse, fine)

    def exchange(value):
        return lax.all_to_all(value, ("inp", "tm"), split_axis=0, concat_axis=0, tiled=True)

    arrived = [exchange(first)]
    for group in range(1, groups):
        value = pl.pallas_call(
            lambda *refs, group=group: transform_kernel(
                *refs, group=group, fine_count=fine_count, owners=owners, steps=steps
            ),
            grid=(steps,),
            in_specs=[frame_spec, *tables],
            out_specs=whole(*piece.shape),
            out_shape=piece,
            scratch_shapes=scratch,
            name="transform",
        )(filtered, coarse, fine)
        arrived.append(exchange(value))

    result = None
    sources = owners
    for group in range(groups):
        value = arrived[group]
        block_inp = inp_count
        if local_inputs % 128:
            value = value.reshape(inp_count, tm_count, 2 * fine_count * steps, local_inputs)
            value = jnp.transpose(value, (1, 2, 0, 3)).reshape(tm_count, 2 * fine_count * steps, all_inputs)
            sources, block_inp = tm_count, 1
        operands = [value] if result is None else [value, result]
        specs = [pl.BlockSpec((sources, 2 * steps, value.shape[2]), lambda c: (0, c, 0))]
        if result is not None:
            specs.append(pl.BlockSpec(memory_space=pl.ANY))
        result = pl.pallas_call(
            lambda *refs, block_inp=block_inp: correlate_kernel(
                *refs, inp_count=block_inp, scale=1.0 / (frame_len * total_spectra)
            ),
            grid=(fine_count,),
            in_specs=specs,
            out_specs=pl.BlockSpec(
                (2, 1, all_inputs, all_inputs), lambda c, group=group: (0, group * fine_count + c, 0, 0)
            ),
            out_shape=jax.ShapeDtypeStruct((2, chan_dev, all_inputs, all_inputs), F32),
            input_output_aliases={} if result is None else {1: 0},
            name="correlate",
        )(*operands)
    return result


def solution(mesh):
    placed = (P("inp", "tm"), P())
    return jax.shard_map(
        on_device,
        mesh=mesh,
        in_specs=placed,
        out_specs=P(None, ("inp", "tm"), None, None),
        check_vma=False,
    )
```

```python
import math

import jax
import jax.numpy as jnp
import numpy as np
from jax import lax
from jax.experimental import pallas as pl
from jax.experimental.pallas import tpu as pltpu
from jax.sharding import PartitionSpec as P


INNER = 4
CHANNEL_STEPS = (8, 4, 4, 6, 6, 4)
HEAD_TERMS = 1
CHUNK = 512
Z_FIRST_GROUPS = 1
F32 = jnp.float32
BF16 = jnp.bfloat16


def next_slice(low, high, count, inner):
    def send(part, pairs):
        return lax.ppermute(part, "tm", pairs)

    via = inner // 2
    edges = range(inner, count, inner)
    detour = via > 0 and len(edges) > 0
    low = send(low, [(d, d + 1) for d in range(count - 1)])
    around = high
    if detour:
        around = send(high, [(d - 1, d + via) for d in edges])
        around = send(around, [(d + via, d) for d in edges])
    high = send(high, [(d, d + 1) for d in range(count - 1) if not detour or (d + 1) % inner])
    return low, high, around if detour else high


def turn_tables(angles, frame_len):
    turn = 2.0 * math.pi / frame_len
    return np.stack([np.cos(angles * turn), np.sin(angles * turn)], axis=-3).astype(np.float32)


def build_table(plane, coarse, fine, table, first_channel, count):
    z_count, _, places, frame_len = coarse.shape
    owners = z_count * places
    rows = count * 2 * owners
    width = min(CHUNK, frame_len)

    def channel(j, _):
        for start in range(0, frame_len, width):
            lanes = pl.ds(start, width)
            cos_c, sin_c = [
                jnp.concatenate([coarse[plane[0] ^ k, f, :, lanes] for k in range(z_count)], axis=0)
                for f in range(2)
            ]
            cos_f, sin_f = [fine[f, pl.ds(first_channel + j, 1), lanes] for f in range(2)]
            parts = (cos_c * cos_f - sin_c * sin_f, -(sin_c * cos_f + cos_c * sin_f))
            for p, exact in enumerate(parts):
                row = pl.multiple_of((2 * j + p) * owners, owners)
                rounded = exact.astype(BF16)
                table[pl.ds(row, owners), lanes] = rounded
                if table.shape[0] == 2 * rows:
                    rest = (exact - rounded.astype(F32)).astype(BF16)
                    table[pl.ds(rows + row, owners), lanes] = rest
        return 0

    lax.fori_loop(0, count, channel, 0)


def transform(frame, table, spread, offset, period, parts):
    contract = (((1,), (1,)), ((), ()))
    spectra = lax.dot_general(table[...], frame, contract, preferred_element_type=F32)
    lanes, length, width = spread.shape
    owners = length // period
    rows = owners * parts
    if spectra.shape[0] == 2 * rows:
        spectra = spectra[:rows] + spectra[rows:]
    for part in range(parts):
        piece = spectra[part * owners : (part + 1) * owners]
        for lane in range(lanes):
            where = pl.ds(offset + 8 * part, owners, stride=period)
            spread[lane, where, :] = piece[:, lane * width : (lane + 1) * width]


def flush(spread, outs):
    lanes, _, width = spread.shape
    views = outs if len(outs) > 1 else [outs[0].at[:, k] for k in range(outs[0].shape[1])]
    places, span, _ = views[0].shape

    def place(i, _):
        for lane in range(lanes):
            for k, view in enumerate(views):
                part = spread[lane, pl.ds(pl.multiple_of((k * places + i) * span, span), span), :]
                view[i, :, lane * width : (lane + 1) * width] = part.astype(BF16)
        return 0

    lax.fori_loop(0, places, place, 0)


def tail_kernel(samples, low, high):
    half = low.shape[0]
    low[...] = samples[:half].astype(F32).astype(BF16)
    high[...] = samples[half:].astype(F32).astype(BF16)


def filter_kernel(plane, *refs, history, count, keep):
    old, refs = refs[:history], refs[history:]
    samples, taps, coarse, fine, filtered, *outs, table, spread, recent, current = refs
    step = pl.program_id(0)
    inputs, frame_len = samples.shape
    width = min(256, frame_len)
    depth = min(16, inputs)

    @pl.when(step == 0)
    def _():
        build_table(plane, coarse, fine, table, 0, count)
        for k in range(keep):
            if history == keep:
                recent[k] = old[k][...].astype(F32).astype(BF16)
                continue
            low, high, around = old[3 * k : 3 * k + 3]
            recent[k, : inputs // 2] = low[...]

            @pl.when(plane[1] == 0)
            def _():
                recent[k, inputs // 2 :] = around[...]

            @pl.when(plane[1] != 0)
            def _():
                recent[k, inputs // 2 :] = high[...]

    slots = [lax.rem(step + k, keep) for k in range(keep)]

    def columns(i, _):
        lanes = pl.ds(pl.multiple_of(i * width, width), width)
        weights = taps[:, lanes].astype(F32) * (1.0 / 16384.0)
        weights = [jnp.broadcast_to(weights[k : k + 1], (depth, width)) for k in range(keep + 1)]
        for start in range(0, inputs, depth):
            here = pl.ds(start, depth)
            newest = samples[here, lanes].astype(F32)
            total = weights[0] * recent[slots[0], here, lanes].astype(F32)
            for k in range(1, keep):
                total = total + weights[k] * recent[slots[k], here, lanes].astype(F32)
            total = total + weights[keep] * newest
            current[here, lanes] = total.astype(BF16)
            recent[slots[0], here, lanes] = newest.astype(BF16)
        return 0

    lax.fori_loop(0, frame_len // width, columns, 0)
    filtered[0] = current[...]
    transform(current[...], table, spread, step, 16 * count, 2 * count)

    @pl.when(step == pl.num_programs(0) - 1)
    def _():
        flush(spread, outs)


def transform_kernel(plane, early, late, coarse, fine, *rest, first_channel, count):
    *outs, table, spread = rest
    step = pl.program_id(0)

    @pl.when(step == 0)
    def _():
        build_table(plane, coarse, fine, table, first_channel, count)

    for half, frame in enumerate((early, late)):
        transform(frame[0], table, spread, 16 * count * half + step, 32 * count, 2 * count)

    @pl.when(step == pl.num_programs(0) - 1)
    def _():
        flush(spread, outs)


def correlate_kernel(*refs, sources, inp_count, scale):
    out = refs[-1]
    parts = []
    for p in range(2):
        pieces = [[] for _ in range(inp_count)]
        for ref in refs[:sources]:
            part = ref[...].astype(F32)[..., 8 * p : 8 * p + 8, :]
            part = part.reshape(inp_count, -1, part.shape[-1])
            for i in range(inp_count):
                pieces[i].append(part[i])
        joined = [jnp.concatenate(each, axis=0) if len(each) > 1 else each[0] for each in pieces]
        whole = jnp.concatenate(joined, axis=1) if inp_count > 1 else joined[0]
        parts.append(whole.astype(BF16))
    real, imag = parts
    real_t, imag_t = real.T, imag.T

    def product(left, right):
        return lax.dot_general(left, right, (((1,), (0,)), ((), ())), preferred_element_type=F32)

    out[0, 0] = (product(real_t, real) + product(imag_t, imag)) * scale
    out[1, 0] = (product(imag_t, real) - product(real_t, imag)) * scale


def on_device(samples, filter_taps):
    local_inputs = samples.shape[0]
    tap_count, frame_len = filter_taps.shape
    steps = samples.shape[1] // frame_len
    channels = frame_len // 2
    inp_count = lax.axis_size("inp")
    tm_count = lax.axis_size("tm")
    inner = math.gcd(INNER, tm_count)
    z_count = tm_count // inner
    places = inp_count * inner
    owners = z_count * places
    all_inputs = local_inputs * inp_count
    chan_dev = channels // owners
    total_spectra = steps * tm_count
    keep = tap_count - 1
    half = steps // 2
    lane_width = min(128, local_inputs)
    lanes = local_inputs // lane_width

    owner_ids = np.arange(owners).reshape(inp_count, z_count, inner).transpose(1, 0, 2).reshape(z_count, places)
    points = np.arange(frame_len)
    coarse = jnp.asarray(turn_tables(owner_ids[..., None] * chan_dev * points % frame_len, frame_len))
    fine = jnp.asarray(turn_tables(np.arange(chan_dev)[:, None] * points % frame_len, frame_len))
    plane = jnp.stack([lax.axis_index("tm") // inner, lax.axis_index("tm") % inner]).astype(jnp.int32)

    head = min(CHANNEL_STEPS[0], chan_dev)
    bounds = [0]
    for number in range(chan_dev):
        if bounds[-1] < chan_dev:
            bounds.append(min(chan_dev, bounds[-1] + CHANNEL_STEPS[min(number, len(CHANNEL_STEPS) - 1)]))
    groups = list(zip(bounds[:-1], bounds[1:]))

    tail_shape = jax.ShapeDtypeStruct((local_inputs // 2, keep * frame_len), BF16)
    tail_spec = pl.BlockSpec((local_inputs // 2, frame_len), lambda s: (0, s))
    tail = pl.pallas_call(
        tail_kernel,
        grid=(keep,),
        in_specs=[pl.BlockSpec((local_inputs, frame_len), lambda s: (0, steps - keep + s))],
        out_specs=[tail_spec, tail_spec],
        out_shape=[tail_shape, tail_shape],
        name="tail",
    )(samples)
    halo = next_slice(*tail, tm_count, inner)
    once = pl.Buffered(1)

    def whole(*shape):
        return pl.BlockSpec(shape, lambda s: (0,) * len(shape), pipeline_mode=once)

    def scratch(count, halves, terms):
        rows = 2 * count * owners
        return [
            pltpu.VMEM((terms * rows, frame_len), BF16),
            pltpu.VMEM((lanes, rows * 8 * halves, lane_width), F32),
        ]

    scalar = pl.BlockSpec(memory_space=pltpu.SMEM)
    tables = [whole(*coarse.shape), whole(*fine.shape)]
    frame_spec = pl.BlockSpec((1, local_inputs, frame_len), lambda s: (s, 0, 0))

    def at_frame(index, count=local_inputs):
        return pl.BlockSpec((count, frame_len), lambda s: (0, index), pipeline_mode=once)

    def filtered_half(first, history, history_specs):
        piece = jax.ShapeDtypeStruct((places, 16 * head, local_inputs), BF16)
        return pl.pallas_call(
            lambda *refs: filter_kernel(*refs, history=len(history), count=head, keep=keep),
            grid=(half,),
            in_specs=[
                scalar,
                *history_specs,
                pl.BlockSpec((local_inputs, frame_len), lambda s: (0, first + s)),
                whole(tap_count, frame_len),
                *tables,
            ],
            out_specs=[frame_spec] + [whole(*piece.shape)] * z_count,
            out_shape=[jax.ShapeDtypeStruct((half, local_inputs, frame_len), BF16)] + [piece] * z_count,
            scratch_shapes=[
                *scratch(head, 1, HEAD_TERMS),
                pltpu.VMEM((keep, local_inputs, frame_len), BF16),
                pltpu.VMEM((local_inputs, frame_len), BF16),
            ],
            name="filter_transform",
        )(plane, *history, samples, filter_taps, coarse, fine)

    def across(value, k):
        pairs = [(z * inner + i, (z ^ k) * inner + i) for z in range(z_count) for i in range(inner)]
        return lax.ppermute(value, "tm", pairs)

    plane_groups = [
        [x * tm_count + z * inner + i for x in range(inp_count) for i in range(inner)] for z in range(z_count)
    ]

    def within(value):
        return lax.all_to_all(
            value, ("inp", "tm"), split_axis=0, concat_axis=0, axis_index_groups=plane_groups, tiled=True
        )

    def z_stage(pieces):
        return [pieces[0]] + [across(pieces[k], k) for k in range(1, z_count)]

    late, *late_pieces = filtered_half(half, [samples] * keep, [at_frame(half - keep + k) for k in range(keep)])
    z_first = z_stage(late_pieces)
    halo_specs = [at_frame(k, local_inputs // 2) for k in range(keep) for _ in range(3)]
    early, *early_pieces = filtered_half(0, list(halo) * keep, halo_specs)
    z_first += z_stage(early_pieces)

    arrived = {}
    z_first_groups = [(0, head, 1, 2 * z_count, 0)]
    for number, (first, last) in enumerate(groups[1:], 2):
        count = last - first
        goes_first = number < 2 + Z_FIRST_GROUPS and 2 * count == head
        if goes_first:
            outs = [jax.ShapeDtypeStruct((places, 32 * count, local_inputs), BF16)] * z_count
        else:
            outs = [jax.ShapeDtypeStruct((places, z_count, 32 * count, local_inputs), BF16)]
        call = pl.pallas_call(
            lambda *refs, first=first, count=count: transform_kernel(*refs, first_channel=first, count=count),
            grid=(half,),
            in_specs=[scalar, frame_spec, frame_spec, *tables],
            out_specs=[whole(*out.shape) for out in outs],
            out_shape=outs,
            scratch_shapes=scratch(count, 2, 2),
            name="transform",
        )
        value = call(plane, early, late, coarse, fine)
        if goes_first:
            z_first_groups.append((first, last, 2, z_count, len(z_first) // z_count))
            z_first += z_stage(value)
        else:
            value = within(value[0])
            moved = [value[:, 0]] + [across(value[:, k], k) for k in range(1, z_count)]
            arrived[first, last] = [
                (each.reshape(places, 1, 2, 16 * count, local_inputs), 1, 0) for each in moved
            ]
    value = within(jnp.stack(z_first, axis=1))
    for first, last, halves, lead, index in z_first_groups:
        shape = (places, len(z_first), halves, value.shape[2] // halves, local_inputs)
        arrived[first, last] = [(value.reshape(shape), lead, index)]

    ready = sorted(arrived)
    plane_first = ready[len(z_first_groups) :]
    order = plane_first[:-2] + ready[: len(z_first_groups)] + plane_first[-2:]
    result = None
    for first, last in order:
        operands, specs = [], []
        block_inp = inp_count
        for value, lead, index in arrived[first, last]:
            if local_inputs % 128:
                block_inp = 1
                value = value.reshape(inp_count, inner, *value.shape[1:])
                value = jnp.transpose(value, (1, 2, 3, 4, 0, 5))
                value = value.reshape(*value.shape[:4], all_inputs)
            operands.append(value)
            block = (value.shape[0], lead, value.shape[2], 16, value.shape[4])
            specs.append(pl.BlockSpec(block, lambda c, index=index: (0, index, 0, c, 0)))
        sources = len(operands)
        if result is not None:
            operands.append(result)
            specs.append(pl.BlockSpec(memory_space=pl.ANY))
        result = pl.pallas_call(
            lambda *refs, block_inp=block_inp, sources=sources: correlate_kernel(
                *refs, sources=sources, inp_count=block_inp, scale=1.0 / (frame_len * total_spectra)
            ),
            grid=(last - first,),
            in_specs=specs,
            out_specs=pl.BlockSpec(
                (2, 1, all_inputs, all_inputs), lambda c, first=first: (0, first + c, 0, 0)
            ),
            out_shape=jax.ShapeDtypeStruct((2, chan_dev, all_inputs, all_inputs), F32),
            input_output_aliases={} if result is None else {sources: 0},
            name="correlate",
        )(*operands)
    return result


def solution(mesh):
    placed = (P("inp", "tm"), P())
    return jax.shard_map(
        on_device,
        mesh=mesh,
        in_specs=placed,
        out_specs=P(None, ("inp", "tm"), None, None),
        check_vma=False,
    )
```

```python
import math

import jax
import jax.numpy as jnp
import numpy as np
from jax import lax
from jax.experimental import pallas as pl
from jax.experimental.pallas import tpu as pltpu
from jax.sharding import PartitionSpec as P


INNER = 4
CHANNEL_STEPS = (8, 4, 4, 4, 7, 5)
HEAD_TERMS = 1
CHUNK = 512
Z_FIRST_GROUPS = 1
F32 = jnp.float32
BF16 = jnp.bfloat16


def next_slice(low, high, count, inner):
    def send(part, pairs):
        return lax.ppermute(part, "tm", pairs)

    via = inner // 2
    edges = range(inner, count, inner)
    detour = via > 0 and len(edges) > 0
    low = send(low, [(d, d + 1) for d in range(count - 1)])
    around = high
    if detour:
        around = send(high, [(d - 1, d + via) for d in edges])
        around = send(around, [(d + via, d) for d in edges])
    high = send(high, [(d, d + 1) for d in range(count - 1) if not detour or (d + 1) % inner])
    if detour:
        high = jnp.where(lax.axis_index("tm") % inner == 0, around, high)
    return low, high


def turn_tables(angles, frame_len):
    turn = 2.0 * math.pi / frame_len
    return np.stack([np.cos(angles * turn), np.sin(angles * turn)], axis=-3).astype(np.float32)


def build_table(plane, coarse, fine, table, first_channel, count):
    z_count, _, places, frame_len = coarse.shape
    owners = z_count * places
    rows = count * 2 * owners
    width = min(CHUNK, frame_len)

    def channel(j, _):
        for start in range(0, frame_len, width):
            lanes = pl.ds(start, width)
            cos_c, sin_c = [
                jnp.concatenate([coarse[plane[0] ^ k, f, :, lanes] for k in range(z_count)], axis=0)
                for f in range(2)
            ]
            cos_f, sin_f = [fine[f, pl.ds(first_channel + j, 1), lanes] for f in range(2)]
            parts = (cos_c * cos_f - sin_c * sin_f, -(sin_c * cos_f + cos_c * sin_f))
            for p, exact in enumerate(parts):
                row = pl.multiple_of((2 * j + p) * owners, owners)
                rounded = exact.astype(BF16)
                table[pl.ds(row, owners), lanes] = rounded
                if table.shape[0] == 2 * rows:
                    rest = (exact - rounded.astype(F32)).astype(BF16)
                    table[pl.ds(rows + row, owners), lanes] = rest
        return 0

    lax.fori_loop(0, count, channel, 0)


def transform(frame, table, spread, offset, period, parts):
    contract = (((1,), (1,)), ((), ()))
    spectra = lax.dot_general(table[...], frame, contract, preferred_element_type=F32)
    lanes, length, width = spread.shape
    owners = length // period
    rows = owners * parts
    if spectra.shape[0] == 2 * rows:
        spectra = spectra[:rows] + spectra[rows:]
    for part in range(parts):
        piece = spectra[part * owners : (part + 1) * owners]
        for lane in range(lanes):
            where = pl.ds(offset + 8 * part, owners, stride=period)
            spread[lane, where, :] = piece[:, lane * width : (lane + 1) * width]


def flush(spread, outs):
    lanes, _, width = spread.shape
    views = outs if len(outs) > 1 else [outs[0].at[:, k] for k in range(outs[0].shape[1])]
    places, span, _ = views[0].shape

    def place(i, _):
        for lane in range(lanes):
            for k, view in enumerate(views):
                part = spread[lane, pl.ds(pl.multiple_of((k * places + i) * span, span), span), :]
                view[i, :, lane * width : (lane + 1) * width] = part.astype(BF16)
        return 0

    lax.fori_loop(0, places, place, 0)


def tail_kernel(samples, low, high):
    half = low.shape[0]
    low[...] = samples[:half].astype(F32).astype(BF16)
    high[...] = samples[half:].astype(F32).astype(BF16)


def filter_kernel(plane, *refs, count, keep):
    old, (samples, taps, coarse, fine), refs = refs[:keep], refs[keep : keep + 4], refs[keep + 4 :]
    if len(refs) > 5 + coarse.shape[0]:
        refs = refs[1:]
    filtered, *outs, table, spread, recent, current = refs
    step = pl.program_id(0)
    inputs, frame_len = samples.shape
    width = min(256, frame_len)
    depth = min(16, inputs)

    @pl.when(step == 0)
    def _():
        build_table(plane, coarse, fine, table, 0, count)
        for k in range(keep):
            recent[k] = old[k][...].astype(F32).astype(BF16)

    slots = [lax.rem(step + k, keep) for k in range(keep)]

    def columns(i, _):
        lanes = pl.ds(pl.multiple_of(i * width, width), width)
        weights = taps[:, lanes].astype(F32) * (1.0 / 16384.0)
        weights = [jnp.broadcast_to(weights[k : k + 1], (depth, width)) for k in range(keep + 1)]
        for start in range(0, inputs, depth):
            here = pl.ds(start, depth)
            newest = samples[here, lanes].astype(F32)
            total = weights[0] * recent[slots[0], here, lanes].astype(F32)
            for k in range(1, keep):
                total = total + weights[k] * recent[slots[k], here, lanes].astype(F32)
            total = total + weights[keep] * newest
            current[here, lanes] = total.astype(BF16)
            recent[slots[0], here, lanes] = newest.astype(BF16)
        return 0

    lax.fori_loop(0, frame_len // width, columns, 0)
    filtered[0] = current[...]
    transform(current[...], table, spread, step, 16 * count, 2 * count)

    @pl.when(step == pl.num_programs(0) - 1)
    def _():
        flush(spread, outs)


def transform_kernel(plane, early, late, coarse, fine, *rest, first_channel, count):
    *outs, table, spread = rest
    step = pl.program_id(0)

    @pl.when(step == 0)
    def _():
        build_table(plane, coarse, fine, table, first_channel, count)

    for half, frame in enumerate((early, late)):
        transform(frame[0], table, spread, 16 * count * half + step, 32 * count, 2 * count)

    @pl.when(step == pl.num_programs(0) - 1)
    def _():
        flush(spread, outs)


def correlate_kernel(*refs, sources, inp_count, scale):
    out = refs[-1]
    parts = []
    for p in range(2):
        pieces = [[] for _ in range(inp_count)]
        for ref in refs[:sources]:
            part = ref[...].astype(F32)[..., 8 * p : 8 * p + 8, :]
            part = part.reshape(inp_count, -1, part.shape[-1])
            for i in range(inp_count):
                pieces[i].append(part[i])
        joined = [jnp.concatenate(each, axis=0) if len(each) > 1 else each[0] for each in pieces]
        whole = jnp.concatenate(joined, axis=1) if inp_count > 1 else joined[0]
        parts.append(whole.astype(BF16))
    real, imag = parts
    real_t, imag_t = real.T, imag.T

    def product(left, right):
        return lax.dot_general(left, right, (((1,), (0,)), ((), ())), preferred_element_type=F32)

    out[0, 0] = (product(real_t, real) + product(imag_t, imag)) * scale
    out[1, 0] = (product(imag_t, real) - product(real_t, imag)) * scale


def on_device(samples, filter_taps):
    local_inputs = samples.shape[0]
    tap_count, frame_len = filter_taps.shape
    steps = samples.shape[1] // frame_len
    channels = frame_len // 2
    inp_count = lax.axis_size("inp")
    tm_count = lax.axis_size("tm")
    inner = math.gcd(INNER, tm_count)
    z_count = tm_count // inner
    places = inp_count * inner
    owners = z_count * places
    all_inputs = local_inputs * inp_count
    chan_dev = channels // owners
    total_spectra = steps * tm_count
    keep = tap_count - 1
    half = steps // 2
    lane_width = min(128, local_inputs)
    lanes = local_inputs // lane_width

    owner_ids = np.arange(owners).reshape(inp_count, z_count, inner).transpose(1, 0, 2).reshape(z_count, places)
    points = np.arange(frame_len)
    coarse = jnp.asarray(turn_tables(owner_ids[..., None] * chan_dev * points % frame_len, frame_len))
    fine = jnp.asarray(turn_tables(np.arange(chan_dev)[:, None] * points % frame_len, frame_len))
    plane = (lax.axis_index("tm") // inner).astype(jnp.int32).reshape(1)

    head = min(CHANNEL_STEPS[0], chan_dev)
    bounds = [0]
    for number in range(chan_dev):
        if bounds[-1] < chan_dev:
            bounds.append(min(chan_dev, bounds[-1] + CHANNEL_STEPS[min(number, len(CHANNEL_STEPS) - 1)]))
    groups = list(zip(bounds[:-1], bounds[1:]))

    tail_shape = jax.ShapeDtypeStruct((local_inputs // 2, keep * frame_len), BF16)
    tail_spec = pl.BlockSpec((local_inputs // 2, frame_len), lambda s: (0, s))
    tail = pl.pallas_call(
        tail_kernel,
        grid=(keep,),
        in_specs=[pl.BlockSpec((local_inputs, frame_len), lambda s: (0, steps - keep + s))],
        out_specs=[tail_spec, tail_spec],
        out_shape=[tail_shape, tail_shape],
        name="tail",
    )(samples)
    halo = next_slice(*tail, tm_count, inner)
    once = pl.Buffered(1)

    def whole(*shape):
        return pl.BlockSpec(shape, lambda s: (0,) * len(shape), pipeline_mode=once)

    def scratch(count, halves, terms):
        rows = 2 * count * owners
        return [
            pltpu.VMEM((terms * rows, frame_len), BF16),
            pltpu.VMEM((lanes, rows * 8 * halves, lane_width), F32),
        ]

    scalar = pl.BlockSpec(memory_space=pltpu.SMEM)
    tables = [whole(*coarse.shape), whole(*fine.shape)]
    frame_spec = pl.BlockSpec((1, local_inputs, frame_len), lambda s: (s, 0, 0))

    parts = 2 if local_inputs % 256 == 0 else 1
    part_inputs = local_inputs // parts

    def filtered_half(first, history, history_block, part, filled):
        piece = jax.ShapeDtypeStruct((places, 16 * head, part_inputs), BF16)
        operands = [plane, *[history] * keep, samples, filter_taps, coarse, fine]
        specs = [
            scalar,
            *[
                pl.BlockSpec(
                    (part_inputs, frame_len),
                    lambda s, k=k: (history_block[0], history_block[1] + k),
                    pipeline_mode=once,
                )
                for k in range(keep)
            ],
            pl.BlockSpec((part_inputs, frame_len), lambda s: (part, first + s)),
            whole(tap_count, frame_len),
            *tables,
        ]
        if filled is not None:
            operands.append(filled)
            specs.append(pl.BlockSpec(memory_space=pl.ANY))
        rows = 2 * head * owners
        return pl.pallas_call(
            lambda *refs: filter_kernel(*refs, count=head, keep=keep),
            grid=(half,),
            in_specs=specs,
            out_specs=[pl.BlockSpec((1, part_inputs, frame_len), lambda s: (s, part, 0))]
            + [whole(*piece.shape)] * z_count,
            out_shape=[jax.ShapeDtypeStruct((half, local_inputs, frame_len), BF16)] + [piece] * z_count,
            scratch_shapes=[
                pltpu.VMEM((HEAD_TERMS * rows, frame_len), BF16),
                pltpu.VMEM((part_inputs // min(128, part_inputs), rows * 8, min(128, part_inputs)), F32),
                pltpu.VMEM((keep, part_inputs, frame_len), BF16),
                pltpu.VMEM((part_inputs, frame_len), BF16),
            ],
            input_output_aliases={} if filled is None else {len(operands) - 1: 0},
            name="filter_transform",
        )(*operands)

    def across(value, k):
        pairs = [(z * inner + i, (z ^ k) * inner + i) for z in range(z_count) for i in range(inner)]
        return lax.ppermute(value, "tm", pairs)

    plane_groups = [
        [x * tm_count + z * inner + i for x in range(inp_count) for i in range(inner)] for z in range(z_count)
    ]

    exchanged = []

    def within(value):
        if exchanged:
            value, _ = lax.optimization_barrier((value, exchanged[-1]))
        moved = lax.all_to_all(
            value, ("inp", "tm"), split_axis=0, concat_axis=0, axis_index_groups=plane_groups, tiled=True
        )
        exchanged.append(moved)
        return moved

    def z_stage(pieces):
        return [pieces[0]] + [across(pieces[k], k) for k in range(1, z_count)]

    def head_half(first, histories, blocks):
        filtered, moved = None, []
        for part in range(parts):
            filtered, *pieces = filtered_half(first, histories[part], blocks[part], part, filtered)
            moved.append(z_stage(pieces))
        return filtered, [jnp.concatenate(each, axis=2) if parts > 1 else each[0] for each in zip(*moved)]

    late, z_first = head_half(half, [samples] * parts, [(part, half - keep) for part in range(parts)])
    if parts == 1:
        halo = [jnp.concatenate(halo, axis=0)]
    early, more = head_half(0, halo, [(0, 0)] * parts)
    z_first += more

    arrived = {}
    z_first_groups = [(0, head, 1, 2 * z_count, 0)]
    for number, (first, last) in enumerate(groups[1:], 2):
        count = last - first
        goes_first = number < 2 + Z_FIRST_GROUPS and 2 * count == head
        if goes_first:
            outs = [jax.ShapeDtypeStruct((places, 32 * count, local_inputs), BF16)] * z_count
        else:
            outs = [jax.ShapeDtypeStruct((places, z_count, 32 * count, local_inputs), BF16)]
        call = pl.pallas_call(
            lambda *refs, first=first, count=count: transform_kernel(*refs, first_channel=first, count=count),
            grid=(half,),
            in_specs=[scalar, frame_spec, frame_spec, *tables],
            out_specs=[whole(*out.shape) for out in outs],
            out_shape=outs,
            scratch_shapes=scratch(count, 2, 2),
            name="transform",
        )
        value = call(plane, early, late, coarse, fine)
        if goes_first:
            z_first_groups.append((first, last, 2, z_count, len(z_first) // z_count))
            z_first += z_stage(value)
        else:
            value = within(value[0])
            moved = [value[:, 0]] + [across(value[:, k], k) for k in range(1, z_count)]
            arrived[first, last] = [
                (each.reshape(places, 1, 2, 16 * count, local_inputs), 1, 0) for each in moved
            ]
    value = within(jnp.stack(z_first, axis=1))
    for first, last, halves, lead, index in z_first_groups:
        shape = (places, len(z_first), halves, value.shape[2] // halves, local_inputs)
        arrived[first, last] = [(value.reshape(shape), lead, index)]

    ready = sorted(arrived)
    plane_first = ready[len(z_first_groups) :]
    order = plane_first[:-2] + ready[: len(z_first_groups)] + plane_first[-2:]
    result = None
    for first, last in order:
        operands, specs = [], []
        block_inp = inp_count
        for value, lead, index in arrived[first, last]:
            if local_inputs % 128:
                block_inp = 1
                value = value.reshape(inp_count, inner, *value.shape[1:])
                value = jnp.transpose(value, (1, 2, 3, 4, 0, 5))
                value = value.reshape(*value.shape[:4], all_inputs)
            operands.append(value)
            block = (value.shape[0], lead, value.shape[2], 16, value.shape[4])
            specs.append(pl.BlockSpec(block, lambda c, index=index: (0, index, 0, c, 0)))
        sources = len(operands)
        if result is not None:
            operands.append(result)
            specs.append(pl.BlockSpec(memory_space=pl.ANY))
        result = pl.pallas_call(
            lambda *refs, block_inp=block_inp, sources=sources: correlate_kernel(
                *refs, sources=sources, inp_count=block_inp, scale=1.0 / (frame_len * total_spectra)
            ),
            grid=(last - first,),
            in_specs=specs,
            out_specs=pl.BlockSpec(
                (2, 1, all_inputs, all_inputs), lambda c, first=first: (0, first + c, 0, 0)
            ),
            out_shape=jax.ShapeDtypeStruct((2, chan_dev, all_inputs, all_inputs), F32),
            input_output_aliases={} if result is None else {sources: 0},
            name="correlate",
        )(*operands)
    return result


def solution(mesh):
    placed = (P("inp", "tm"), P())
    return jax.shard_map(
        on_device,
        mesh=mesh,
        in_specs=placed,
        out_specs=P(None, ("inp", "tm"), None, None),
        check_vma=False,
    )
```
